128 devices in a mesh: ao: 8 (over y, x_hi), prow: 8 (over z, core), pcol: 2 (over x_lo).
Axes of the slice: x: 4 (x_hi: 2, x_lo: 2; x = x_hi * 2 + x_lo), y: 4, z: 4, core: 2. Of those that a mesh axis runs over, the one named last changes fastest.
Arguments:
- three_index: bfloat16 [1024, 1200, 1200], P(('prow', 'pcol'), 'ao'), may hold values from -1.0546875 to 1.0546875
- coefficients: bfloat16 [1200, 120], replicated, may hold values from -0.1875 to 0.1875
Outputs:
- coulomb: bfloat16 [14400, 14400], P('ao', ('prow', 'pcol'))
The draws below stay inside these ranges and needn't reach their ends.
All inputs are finite; a program needn't handle non-finite values.
Results may differ from the reference program's by a relative error of at most 0.0069.
Values may be sent and summed in bfloat16 or wider, within the bound.
No kernel may reach another device: no remote copies, remote signals or barrier semaphores. Data moves between devices by JAX's collectives and lax.ppermute only.
A program may use at most 192 MiB of HBM per device.

```python
import jax
import jax.numpy as jnp
from jax import lax

N = 1200
A = 120
AUX_DEV = 64
AUX = 1024


def block_scale(stream_key, extent, cuts, least, largest):
    gain, own = 1.0, jax.random.fold_in(stream_key, 6)
    for axis_at, blocks in cuts:
        heights = jnp.exp(jax.random.uniform(jax.random.fold_in(own, axis_at), (blocks,), jnp.float32, least / len(cuts), largest / len(cuts)))
        gain = gain * jnp.repeat(heights, extent[axis_at] // blocks).reshape([-1 if axis == axis_at else 1 for axis in range(len(extent))])
    return gain


def centred(key, extent, width, limit, cuts=(), dtype=jnp.bfloat16):
    drawn = jax.random.normal(key, extent, jnp.float32) * width
    if len(cuts) > 0:
        drawn = block_scale(key, extent, cuts, -0.22, 0.18) * drawn
    return jnp.clip(drawn, min=-limit, max=limit).astype(dtype)


def setup_inputs(seed: int = 0) -> dict:
    keys = jax.random.split(jax.random.key(seed), 3)
    return {
        "three_index": centred(keys[0], (AUX, N, N), (AUX ** -0.25), 1.0546875, ((0, 16), (1, 8))),
        "coefficients": centred(keys[1], (N, A), N ** -0.5, 0.1875),
    }


def reference(three_index, coefficients):
    def transform(block):
        half = jnp.dot(block.reshape(-1, N), coefficients, preferred_element_type=jnp.float32)
        half = half.astype(jnp.bfloat16).reshape(-1, N, A)
        summed = jnp.einsum("mp,amq->apq", coefficients.astype(jnp.float32), half.astype(jnp.float32))
        return summed.reshape(-1, A * A).astype(jnp.bfloat16)

    blocks = three_index.reshape(AUX // AUX_DEV, AUX_DEV, N, N)
    pair_ints = lax.map(transform, blocks).reshape(AUX, A * A)
    coulomb = lax.dot_general(pair_ints, pair_ints, (((0,), (0,)), ((), ())), preferred_element_type=jnp.float32)
    return coulomb.astype(jnp.bfloat16)
```

```python
import functools

import jax
import jax.numpy as jnp
from jax import lax
from jax.experimental import pallas as pl
from jax.experimental.pallas import tpu as pltpu
from jax.sharding import PartitionSpec as P


AXES = ("ao", "prow", "pcol")
STEPS = (1, 3, 2)
SLOTS = (
    ((0, 0), (0, 1), (1, 0), (1, 1), (3, 0), (3, 1), (2, 0), (2, 1)),
    ((0, 0), (1, 0), (0, 1), (1, 1), (2, 1), (3, 1), (2, 0), (3, 0)),
)


def place():
    ao, prow = lax.axis_index("ao"), lax.axis_index("prow")
    return ao // 2, lax.rem(ao, 2), prow // 2, lax.rem(prow, 2), lax.axis_index("pcol")


def send(value, to):
    pairs = []
    for y in range(4):
        for xh in range(2):
            for z in range(4):
                for k in range(2):
                    for xl in range(2):
                        y2, xh2, z2, k2, xl2 = to(y, xh, z, k, xl)
                        source = ((y * 2 + xh) * 8 + z * 2 + k) * 2 + xl
                        target = ((y2 % 4 * 2 + xh2 % 2) * 8 + z2 % 4 * 2 + k2 % 2) * 2 + xl2 % 2
                        pairs.append((source, target))
    return lax.ppermute(value, AXES, pairs)


def pairs_kernel(block_ref, coef_ref, own_ref, *rest, rows, group, active, per):
    outs, (half, ints) = rest[:4], rest[4:]
    y, xh, _, core, _ = place()
    basis = block_ref.shape[2]
    half[:, :active] = jnp.dot(
        block_ref[...].reshape(rows * group, basis),
        coef_ref[...],
        preferred_element_type=jnp.float32,
    )
    wide = jnp.concatenate(
        [half[pl.ds(p, rows, stride=group), :].astype(jnp.bfloat16) for p in range(group)], axis=1
    )
    product = jnp.dot(own_ref[...], wide, preferred_element_type=jnp.float32)
    for p in range(group):
        ints[p * active : (p + 1) * active, :] = product[:, p * 128 : (p + 1) * 128]
    for slot in range(8):
        (dy0, dx0), (dy1, dx1) = SLOTS[0][slot], SLOTS[1][slot]
        dy = dy0 + core * (dy1 - dy0)
        dx = dx0 + core * (dx1 - dx0)
        first = (lax.rem(y + dy, 4) * 2 + lax.rem(xh + dx, 2)) * per
        pieces = [ints[pl.ds(first + j, group, stride=active), :][:, :active] for j in range(per)]
        outs[slot // 2][slot % 2] = jnp.concatenate(pieces, axis=1).astype(jnp.bfloat16)


def pair_terms(three_index, coefficients, group=8):
    block = jnp.transpose(three_index, (1, 0, 2))
    rows, aux, basis = block.shape
    active = coefficients.shape[1]
    per = active // 8
    own = lax.dynamic_slice_in_dim(coefficients, lax.axis_index("ao") * rows, rows, 0).T
    message = jax.ShapeDtypeStruct((2, aux, per * active), jnp.bfloat16)
    once = pl.Buffered(1)
    return pl.pallas_call(
        functools.partial(pairs_kernel, rows=rows, group=group, active=active, per=per),
        out_shape=(message,) * 4,
        grid=(aux // group,),
        in_specs=[
            pl.BlockSpec((rows, group, basis), lambda i: (0, i, 0)),
            pl.BlockSpec((basis, active), lambda i: (0, 0), pipeline_mode=once),
            pl.BlockSpec((active, rows), lambda i: (0, 0), pipeline_mode=once),
        ],
        out_specs=(pl.BlockSpec((2, group, per * active), lambda i: (0, i, 0)),) * 4,
        scratch_shapes=[
            pltpu.VMEM((rows * group, 128), jnp.float32),
            pltpu.VMEM((group * active, 128), jnp.float32),
        ],
        name="pair_terms",
    )(block, coefficients, own)


def sum_scatter(messages):
    f32 = lambda v: v.astype(jnp.float32)
    core = lax.rem(lax.axis_index("prow"), 2)

    def first(j):
        def to(y, xh, z, k, xl):
            if k == 0:
                return y + STEPS[j], xh, z, k, xl
            return y, xh + (j < 2), z, k, xl

        return to

    def second(j):
        def to(y, xh, z, k, xl):
            if k == 1:
                return y + STEPS[j], xh, z, k, xl
            return y, xh + (j < 1), z, k, xl

        return to

    got = [send(messages[j + 1], first(j)) for j in range(3)]
    near = f32(messages[0]) + f32(got[0])
    near = jnp.where(core == 0, near + f32(got[1]) + f32(got[2]), near)
    far = f32(messages[3]) + f32(got[1])
    got = [
        send(near[1].astype(jnp.bfloat16), second(0)),
        send(far[1].astype(jnp.bfloat16), second(1)),
        send(far[0].astype(jnp.bfloat16), second(2)),
    ]
    total = near[0] + f32(got[0])
    return jnp.where(core == 0, total, total + f32(got[1]) + f32(got[2])).astype(jnp.bfloat16)


def row_panel(block):
    across = send(block, lambda y, xh, z, k, xl: (y, xh, z, k, xl + 1))
    pieces, where = [block, across], [(0, 0), (0, 1)]
    for piece, flip in ((block, 0), (across, 1)):
        for d in STEPS:
            pieces.append(send(piece, lambda y, xh, z, k, xl, d=d: (y, xh, z + d, k, xl)))
            where.append((d, flip))
    twins = [send(piece, lambda y, xh, z, k, xl: (y, xh, z, k + 1, xl)) for piece in pieces]

    def numbers(y, xh, z, k, xl):
        mine = [lax.rem(z + 4 - d, 4) * 4 + lax.rem(xl + flip, 2) for d, flip in where]
        return [n + 2 * k for n in mine] + [n + 2 * (1 - k) for n in mine]

    return pieces + twins, numbers


def column_panel(block):
    width = block.shape[1] // 2
    xl = lax.axis_index("pcol")
    left, right = block[:, :width], block[:, width:]
    same = send(
        jnp.where(xl == 0, left, right), lambda y, xh, z, k, xl: (2 * y - z, k, y, xh, xl)
    )
    other = send(
        jnp.where(xl == 0, right, left), lambda y, xh, z, k, xl: (2 * y - z, k, y, xh, xl + 1)
    )
    both = jnp.stack([same, other])
    across = send(both, lambda y, xh, z, k, xl: (y, xh + 1, z, k, xl))
    pieces, where = [both, across], [(0, 0), (0, 1)]
    for piece, flip in ((both, 0), (across, 1)):
        for d in STEPS:
            pieces.append(send(piece, lambda y, xh, z, k, xl, d=d: (y + d, xh, z, k, xl)))
            where.append((d, flip))

    def numbers(y, xh, z, k, xl):
        out = []
        for d, flip in where:
            base = lax.rem(2 * z + 4 - y + d, 4) * 4 + 2 * lax.rem(xh + flip, 2)
            out.append((base + xl, base + 1 - xl))
        return out

    return pieces, numbers


def product_kernel(*refs, n_rows, n_cols, row_numbers, column_numbers, tile):
    row_refs, col_refs = refs[:n_rows], refs[n_rows : n_rows + n_cols]
    out_ref, rows, cols, stage, row_sem, col_sem, out_sem = refs[n_rows + n_cols :]
    here = place()
    copies = []
    for i, (ref, number) in enumerate(zip(row_refs, row_numbers(*here))):
        copies.append(pltpu.make_async_copy(ref, rows.at[number], row_sem.at[i]))
    for i, (ref, numbers) in enumerate(zip(col_refs, column_numbers(*here))):
        for j, number in enumerate(numbers):
            copies.append(pltpu.make_async_copy(ref.at[j], cols.at[number], col_sem.at[2 * i + j]))
    for copy in copies:
        copy.start()
    for copy in copies:
        copy.wait()
    depth = rows.shape[0] * rows.shape[1]
    width = cols.shape[2]
    right = rows[...].reshape(depth, rows.shape[2])
    stores = []
    for t, start in enumerate(range(0, width, tile)):
        stop = min(start + tile, width)
        left = cols[:, :, start:stop].reshape(depth, stop - start)
        stage[start:stop] = lax.dot_general(
            left, right, (((0,), (0,)), ((), ())), preferred_element_type=jnp.float32
        ).astype(jnp.bfloat16)
        stores.append(
            pltpu.make_async_copy(stage.at[start:stop], out_ref.at[start:stop], out_sem.at[t])
        )
        stores[-1].start()
    for store in stores:
        store.wait()


def product(rows, row_numbers, cols, column_numbers, tile=256):
    aux, height = rows[0].shape
    width = cols[0].shape[2]
    blocks = len(rows)
    anywhere = pl.BlockSpec(memory_space=pl.ANY)
    return pl.pallas_call(
        functools.partial(
            product_kernel,
            n_rows=len(rows),
            n_cols=len(cols),
            row_numbers=row_numbers,
            column_numbers=column_numbers,
            tile=tile,
        ),
        out_shape=jax.ShapeDtypeStruct((width, height), jnp.bfloat16),
        in_specs=[anywhere] * (len(rows) + len(cols)),
        out_specs=anywhere,
        scratch_shapes=[
            pltpu.VMEM((blocks, aux, height), jnp.bfloat16),
            pltpu.VMEM((blocks, aux, width), jnp.bfloat16),
            pltpu.VMEM((width, height), jnp.bfloat16),
            pltpu.SemaphoreType.DMA((len(rows),)),
            pltpu.SemaphoreType.DMA((2 * len(cols),)),
            pltpu.SemaphoreType.DMA((-(-width // tile),)),
        ],
        name="product",
    )(*rows, *cols).T


def on_device(three_index, coefficients):
    block = sum_scatter(pair_terms(three_index, coefficients))
    cols, column_numbers = column_panel(block)
    rows, row_numbers = row_panel(block)
    return product(rows, row_numbers, cols, column_numbers)


def solution(mesh):
    placed = (P(("prow", "pcol"), "ao", None), P())
    return jax.shard_map(
        on_device, mesh=mesh, in_specs=placed, out_specs=P("ao", ("prow", "pcol")), check_vma=False
    )
```

```python
import functools

import jax
import jax.numpy as jnp
from jax import lax
from jax.experimental import pallas as pl
from jax.experimental.pallas import tpu as pltpu
from jax.sharding import PartitionSpec as P


AXES = ("ao", "prow", "pcol")
STEPS = (2, 1, 3)
SLOTS = (
    ((0, 0), (0, 1), (2, 0), (2, 1), (1, 0), (1, 1), (3, 0), (3, 1)),
    ((0, 0), (2, 0), (0, 1), (2, 1), (3, 1), (1, 1), (3, 0), (1, 0)),
)


def place():
    ao, prow = lax.axis_index("ao"), lax.axis_index("prow")
    return ao // 2, lax.rem(ao, 2), prow // 2, lax.rem(prow, 2), lax.axis_index("pcol")


def send(value, to):
    pairs = []
    for y in range(4):
        for xh in range(2):
            for z in range(4):
                for k in range(2):
                    for xl in range(2):
                        y2, xh2, z2, k2, xl2 = to(y, xh, z, k, xl)
                        source = ((y * 2 + xh) * 8 + z * 2 + k) * 2 + xl
                        target = ((y2 % 4 * 2 + xh2 % 2) * 8 + z2 % 4 * 2 + k2 % 2) * 2 + xl2 % 2
                        pairs.append((source, target))
    return lax.ppermute(value, AXES, pairs)


def pairs_kernel(block_ref, coef_ref, *rest, rows, group, active, per, steps):
    outs, (half_a, half_b, ints, wide_coef, own) = rest[:4], rest[4:]
    y, xh, _, core, _ = place()
    basis = block_ref.shape[2]
    step = pl.program_id(0)

    @pl.when(step == 0)
    def _():
        wide_coef[:basis, :active] = coef_ref[...].astype(jnp.float32)
        mine = wide_coef[pl.ds((2 * y + xh) * rows, 256), :]
        own[...] = mine.T[:active, :rows].astype(jnp.bfloat16)

    def first(half):
        half[:, :active] = jnp.dot(
            block_ref[...].reshape(rows * group, basis),
            coef_ref[...],
            preferred_element_type=jnp.float32,
        )

    def second(half):
        wide = jnp.concatenate(
            [half[pl.ds(p, rows, stride=group), :].astype(jnp.bfloat16) for p in range(group)],
            axis=1,
        )
        product = jnp.dot(own[...], wide, preferred_element_type=jnp.float32)
        for p in range(group):
            ints[p * active : (p + 1) * active, :] = product[:, p * 128 : (p + 1) * 128]
        for slot in range(8):
            (dy0, dx0), (dy1, dx1) = SLOTS[0][slot], SLOTS[1][slot]
            dy = dy0 + core * (dy1 - dy0)
            dx = dx0 + core * (dx1 - dx0)
            start = (lax.rem(y + dy, 4) * 2 + lax.rem(xh + dx, 2)) * per
            pieces = [ints[pl.ds(start + j, group, stride=active), :][:, :active] for j in range(per)]
            outs[slot // 2][slot % 2] = jnp.concatenate(pieces, axis=1).astype(jnp.bfloat16)

    even = lax.rem(step, 2) == 0

    @pl.when(step == 0)
    def _():
        first(half_a)

    @pl.when((step > 0) & (step < steps) & jnp.logical_not(even))
    def _():
        first(half_b)
        second(half_a)

    @pl.when((step > 0) & (step < steps) & even)
    def _():
        first(half_a)
        second(half_b)

    @pl.when(step == steps)
    def _():
        second(half_b if steps % 2 == 0 else half_a)


def pair_terms(three_index, coefficients, group=16):
    block = jnp.transpose(three_index, (1, 0, 2))
    rows, aux, basis = block.shape
    active = coefficients.shape[1]
    per = active // 8
    steps = aux // group
    message = jax.ShapeDtypeStruct((2, aux, per * active), jnp.bfloat16)
    half = pltpu.VMEM((rows * group, 128), jnp.float32)
    return pl.pallas_call(
        functools.partial(
            pairs_kernel, rows=rows, group=group, active=active, per=per, steps=steps
        ),
        out_shape=(message,) * 4,
        grid=(steps + 1,),
        in_specs=[
            pl.BlockSpec((rows, group, basis), lambda i: (0, jnp.minimum(i, steps - 1), 0)),
            pl.BlockSpec((basis, active), lambda i: (0, 0), pipeline_mode=pl.Buffered(1)),
        ],
        out_specs=(
            pl.BlockSpec((2, group, per * active), lambda i: (0, jnp.maximum(i - 1, 0), 0)),
        )
        * 4,
        scratch_shapes=[
            half,
            half,
            pltpu.VMEM((group * active, 128), jnp.float32),
            pltpu.VMEM((7 * rows + 256 + 6, 128), jnp.float32),
            pltpu.VMEM((active, rows), jnp.bfloat16),
        ],
        compiler_params=pltpu.CompilerParams(vmem_limit_bytes=32 << 20),
        name="pair_terms",
    )(block, coefficients)


def sum_scatter(messages):
    f32 = lambda v: v.astype(jnp.float32)
    core = lax.rem(lax.axis_index("prow"), 2)

    def first(j):
        def to(y, xh, z, k, xl):
            if k == 0:
                return y + STEPS[j], xh, z, k, xl
            return y, xh + (j < 2), z, k, xl

        return to

    def second(j):
        def to(y, xh, z, k, xl):
            if k == 1:
                return y + STEPS[j], xh, z, k, xl
            return y, xh + (j < 1), z, k, xl

        return to

    got = [send(messages[j + 1], first(j)) for j in range(3)]
    near = f32(messages[0]) + f32(got[0])
    near = jnp.where(core == 0, near + f32(got[1]) + f32(got[2]), near)
    far = f32(messages[3]) + f32(got[1])
    got = [
        send(near[1].astype(jnp.bfloat16), second(0)),
        send(far[1].astype(jnp.bfloat16), second(1)),
        send(far[0].astype(jnp.bfloat16), second(2)),
    ]
    total = near[0] + f32(got[0])
    return jnp.where(core == 0, total, total + f32(got[1]) + f32(got[2])).astype(jnp.bfloat16)


def row_panel(block):
    across = send(block, lambda y, xh, z, k, xl: (y, xh, z, k, xl + 1))
    mine = {(0, 0): block, (0, 1): across}
    for flip, piece in ((0, block), (1, across)):
        for d in STEPS[flip:]:
            mine[d, flip] = send(piece, lambda y, xh, z, k, xl, d=d: (y, xh, z + d, k, xl))
    mine[2, 1] = send(mine[2, 0], lambda y, xh, z, k, xl: (y, xh, z, k, xl + 1))
    twins = []
    for d, flip in sorted(mine):
        twins.append(send(mine[d, flip], lambda y, xh, z, k, xl: (y, xh, z, k + 1, xl)))
    return [mine[key] for key in sorted(mine)] + twins


def column_panel(block):
    width = block.shape[1] // 2
    xl = lax.axis_index("pcol")
    left, right = block[:, :width], block[:, width:]
    same = send(
        jnp.where(xl == 0, left, right), lambda y, xh, z, k, xl: (2 * y - z + 2, k, y, xh, xl)
    )
    other = send(
        jnp.where(xl == 0, right, left), lambda y, xh, z, k, xl: (2 * y - z + 2, k, y, xh, xl + 1)
    )
    both = jnp.stack([same, other])
    across = send(both, lambda y, xh, z, k, xl: (y, xh + 1, z, k, xl))
    mine = {(0, 0): both, (0, 1): across}
    for flip, piece in ((0, both), (1, across)):
        for d in STEPS[flip:]:
            mine[d, flip] = send(piece, lambda y, xh, z, k, xl, d=d: (y + d, xh, z, k, xl))
    mine[2, 1] = send(mine[2, 0], lambda y, xh, z, k, xl: (y, xh + 1, z, k, xl))
    return [mine[key] for key in sorted(mine)]


def product_kernel(*refs, tile):
    row_refs, col_refs = refs[:16], refs[16:24]
    out_ref, cols, stage, out_sem = refs[24:]
    y, xh, z, k, _ = place()
    where = [(d, flip) for d in range(4) for flip in range(2)]
    for ref, (d, flip) in zip(col_refs, where):
        base = 2 * lax.rem(y + 6 - d - z, 4) + 8 * lax.rem(xh + flip + k, 2)
        for j in range(2):
            cols[base + j] = ref[j]
    _, aux, width = cols.shape
    right = jnp.concatenate([ref[...] for ref in row_refs], axis=0)
    stores = []
    for t, start in enumerate(range(0, width, tile)):
        stop = min(start + tile, width)
        left = cols[:, :, start:stop].reshape(16 * aux, stop - start)
        stage[start:stop] = lax.dot_general(
            left, right, (((0,), (0,)), ((), ())), preferred_element_type=jnp.float32
        ).astype(jnp.bfloat16)
        stores.append(
            pltpu.make_async_copy(stage.at[start:stop], out_ref.at[start:stop], out_sem.at[t])
        )
        stores[-1].start()
    for store in stores:
        store.wait()


def product(rows, cols, tile=256):
    aux, height = rows[0].shape
    width = cols[0].shape[2]
    inside = pl.BlockSpec(memory_space=pltpu.VMEM)
    return pl.pallas_call(
        functools.partial(product_kernel, tile=tile),
        out_shape=jax.ShapeDtypeStruct((width, height), jnp.bfloat16),
        in_specs=[inside] * (len(rows) + len(cols)),
        out_specs=pl.BlockSpec(memory_space=pl.ANY),
        scratch_shapes=[
            pltpu.VMEM((16, aux, width), jnp.bfloat16),
            pltpu.VMEM((width, height), jnp.bfloat16),
            pltpu.SemaphoreType.DMA((-(-width // tile),)),
        ],
        compiler_params=pltpu.CompilerParams(vmem_limit_bytes=32 << 20),
        name="product",
    )(*rows, *cols).T


def on_device(three_index, coefficients):
    block = sum_scatter(pair_terms(three_index, coefficients))
    return product(row_panel(block), column_panel(block))


def solution(mesh):
    placed = (P(("prow", "pcol"), "ao", None), P())
    return jax.shard_map(
        on_device, mesh=mesh, in_specs=placed, out_specs=P("ao", ("prow", "pcol")), check_vma=False
    )
```

```python
import functools

import jax
import jax.numpy as jnp
from jax import lax
from jax.experimental import pallas as pl
from jax.experimental.pallas import tpu as pltpu
from jax.sharding import PartitionSpec as P


AXES = ("ao", "prow", "pcol")
STEPS = (2, 1, 3)
SLOTS = (
    ((0, 0), (0, 1), (2, 0), (2, 1), (1, 0), (1, 1), (3, 0), (3, 1)),
    ((0, 0), (2, 0), (0, 1), (2, 1), (3, 1), (1, 1), (3, 0), (1, 0)),
)


def place():
    ao, prow = lax.axis_index("ao"), lax.axis_index("prow")
    return ao // 2, lax.rem(ao, 2), prow // 2, lax.rem(prow, 2), lax.axis_index("pcol")


def send(value, to):
    pairs = []
    for y in range(4):
        for xh in range(2):
            for z in range(4):
                for k in range(2):
                    for xl in range(2):
                        y2, xh2, z2, k2, xl2 = to(y, xh, z, k, xl)
                        source = ((y * 2 + xh) * 8 + z * 2 + k) * 2 + xl
                        target = ((y2 % 4 * 2 + xh2 % 2) * 8 + z2 % 4 * 2 + k2 % 2) * 2 + xl2 % 2
                        pairs.append((source, target))
    return lax.ppermute(value, AXES, pairs)


def pairs_kernel(block_ref, coef_ref, *rest, rows, group, active, per, steps):
    outs, (half_a, half_b, ints, wide_coef, own) = rest[:4], rest[4:]
    y, xh, _, core, _ = place()
    basis = block_ref.shape[2]
    step = pl.program_id(0)

    @pl.when(step == 0)
    def _():
        wide_coef[:basis, :active] = coef_ref[...].astype(jnp.float32)
        mine = wide_coef[pl.ds((2 * y + xh) * rows, 256), :]
        own[...] = mine.T[:active, :rows].astype(jnp.bfloat16)

    def first(half):
        half[:, :active] = jnp.dot(
            block_ref[...].reshape(rows * group, basis),
            coef_ref[...],
            preferred_element_type=jnp.float32,
        )

    def second(half):
        wide = jnp.concatenate(
            [half[pl.ds(p, rows, stride=group), :].astype(jnp.bfloat16) for p in range(group)],
            axis=1,
        )
        product = jnp.dot(own[...], wide, preferred_element_type=jnp.float32)
        for p in range(group):
            ints[p * active : (p + 1) * active, :] = product[:, p * 128 : (p + 1) * 128]
        for slot in range(8):
            (dy0, dx0), (dy1, dx1) = SLOTS[0][slot], SLOTS[1][slot]
            dy = dy0 + core * (dy1 - dy0)
            dx = dx0 + core * (dx1 - dx0)
            start = (lax.rem(y + dy, 4) * 2 + lax.rem(xh + dx, 2)) * per
            pieces = [ints[pl.ds(start + j, group, stride=active), :][:, :active] for j in range(per)]
            outs[slot // 2][slot % 2] = jnp.concatenate(pieces, axis=1).astype(jnp.bfloat16)

    even = lax.rem(step, 2) == 0

    @pl.when(step == 0)
    def _():
        first(half_a)

    @pl.when((step > 0) & (step < steps) & jnp.logical_not(even))
    def _():
        first(half_b)
        second(half_a)

    @pl.when((step > 0) & (step < steps) & even)
    def _():
        first(half_a)
        second(half_b)

    @pl.when(step == steps)
    def _():
        second(half_b if steps % 2 == 0 else half_a)


def pair_terms(three_index, coefficients, group=16):
    block = jnp.transpose(three_index, (1, 0, 2))
    rows, aux, basis = block.shape
    active = coefficients.shape[1]
    per = active // 8
    steps = aux // group
    message = jax.ShapeDtypeStruct((2, aux, per * active), jnp.bfloat16)
    half = pltpu.VMEM((rows * group, 128), jnp.float32)
    return pl.pallas_call(
        functools.partial(
            pairs_kernel, rows=rows, group=group, active=active, per=per, steps=steps
        ),
        out_shape=(message,) * 4,
        grid=(steps + 1,),
        in_specs=[
            pl.BlockSpec((rows, group, basis), lambda i: (0, jnp.minimum(i, steps - 1), 0)),
            pl.BlockSpec((basis, active), lambda i: (0, 0), pipeline_mode=pl.Buffered(1)),
        ],
        out_specs=(
            pl.BlockSpec((2, group, per * active), lambda i: (0, jnp.maximum(i - 1, 0), 0)),
        )
        * 4,
        scratch_shapes=[
            half,
            half,
            pltpu.VMEM((group * active, 128), jnp.float32),
            pltpu.VMEM((7 * rows + 256 + 6, 128), jnp.float32),
            pltpu.VMEM((active, rows), jnp.bfloat16),
        ],
        compiler_params=pltpu.CompilerParams(vmem_limit_bytes=32 << 20),
        name="pair_terms",
    )(block, pltpu.with_memory_space_constraint(coefficients, pltpu.HBM))


def sum_scatter(messages):
    f32 = lambda v: v.astype(jnp.float32)
    core = lax.rem(lax.axis_index("prow"), 2)

    def first(j):
        def to(y, xh, z, k, xl):
            if k == 0:
                return y + STEPS[j], xh, z, k, xl
            return y, xh + (j < 2), z, k, xl

        return to

    def second(j):
        def to(y, xh, z, k, xl):
            if k == 1:
                return y + STEPS[j], xh, z, k, xl
            return y, xh + (j < 1), z, k, xl

        return to

    got = [send(messages[j + 1], first(j)) for j in range(3)]
    near = f32(messages[0]) + f32(got[0])
    near = jnp.where(core == 0, near + f32(got[1]) + f32(got[2]), near)
    far = f32(messages[3]) + f32(got[1])
    got = [
        send(near[1].astype(jnp.bfloat16), second(0)),
        send(far[1].astype(jnp.bfloat16), second(1)),
        send(far[0].astype(jnp.bfloat16), second(2)),
    ]
    total = near[0] + f32(got[0])
    return jnp.where(core == 0, total, total + f32(got[1]) + f32(got[2])).astype(jnp.bfloat16)


def row_panel(block):
    across = send(block, lambda y, xh, z, k, xl: (y, xh, z, k, xl + 1))
    mine = {(0, 0): block, (0, 1): across}
    for flip, piece in ((0, block), (1, across)):
        for d in STEPS[flip:]:
            mine[d, flip] = send(piece, lambda y, xh, z, k, xl, d=d: (y, xh, z + d, k, xl))
    mine[2, 1] = send(mine[2, 0], lambda y, xh, z, k, xl: (y, xh, z, k, xl + 1))
    twins = []
    for d, flip in sorted(mine):
        twins.append(send(mine[d, flip], lambda y, xh, z, k, xl: (y, xh, z, k + 1, xl)))
    return [mine[key] for key in sorted(mine)] + twins


def column_panel(block):
    width = block.shape[1] // 2
    xl = lax.axis_index("pcol")
    left, right = block[:, :width], block[:, width:]
    core = lax.rem(lax.axis_index("prow"), 2)
    keep = xl == core

    def turn(first):
        def to(y, xh, z, k, xl):
            flip = (k + first) % 2
            return 2 * y - z + 2, xh + flip, y, xh, xl + flip

        return to

    same = send(jnp.where(keep, left, right), turn(0))
    other = send(jnp.where(keep, right, left), turn(1))
    both = jnp.stack([same, other])
    across = send(both, lambda y, xh, z, k, xl: (y, xh + 1, z, k, xl))
    mine = {(0, 0): both, (0, 1): across}
    for flip, piece in ((0, both), (1, across)):
        for d in STEPS[flip:]:
            mine[d, flip] = send(piece, lambda y, xh, z, k, xl, d=d: (y + d, xh, z, k, xl))
    mine[2, 1] = send(mine[2, 0], lambda y, xh, z, k, xl: (y, xh + 1, z, k, xl))
    return [mine[key] for key in sorted(mine)]


def product_kernel(*refs, tile):
    row_refs, col_refs = refs[:16], refs[16:24]
    out_ref, cols, stage, out_sem = refs[24:]
    y, xh, z, k, _ = place()
    where = [(d, flip) for d in range(4) for flip in range(2)]
    for ref, (d, flip) in zip(col_refs, where):
        kind = lax.rem(xh + flip + k, 2)
        base = 2 * lax.rem(y + 6 - d - z, 4) + kind
        for j in range(2):
            cols[base + 8 * lax.rem(j + kind + k, 2)] = ref[j]
    _, aux, width = cols.shape
    right = jnp.concatenate([ref[...] for ref in row_refs], axis=0)
    stores = []
    for t, start in enumerate(range(0, width, tile)):
        stop = min(start + tile, width)
        left = cols[:, :, start:stop].reshape(16 * aux, stop - start)
        stage[start:stop] = lax.dot_general(
            left, right, (((0,), (0,)), ((), ())), preferred_element_type=jnp.float32
        ).astype(jnp.bfloat16)
        stores.append(
            pltpu.make_async_copy(stage.at[start:stop], out_ref.at[start:stop], out_sem.at[t])
        )
        stores[-1].start()
    for store in stores:
        store.wait()


def product(rows, cols, tile=384):
    aux, height = rows[0].shape
    width = cols[0].shape[2]
    inside = pl.BlockSpec(memory_space=pltpu.VMEM)
    return pl.pallas_call(
        functools.partial(product_kernel, tile=tile),
        out_shape=jax.ShapeDtypeStruct((width, height), jnp.bfloat16),
        in_specs=[inside] * (len(rows) + len(cols)),
        out_specs=pl.BlockSpec(memory_space=pl.ANY),
        scratch_shapes=[
            pltpu.VMEM((16, aux, width), jnp.bfloat16),
            pltpu.VMEM((width, height), jnp.bfloat16),
            pltpu.SemaphoreType.DMA((-(-width // tile),)),
        ],
        compiler_params=pltpu.CompilerParams(vmem_limit_bytes=32 << 20),
        name="product",
    )(*rows, *cols).T


def on_device(three_index, coefficients):
    block = sum_scatter(pair_terms(three_index, coefficients))
    return product(row_panel(block), column_panel(block))


def solution(mesh):
    placed = (P(("prow", "pcol"), "ao", None), P())
    return jax.shard_map(
        on_device, mesh=mesh, in_specs=placed, out_specs=P("ao", ("prow", "pcol")), check_vma=False
    )
```
